32 devices in a mesh: dp: 8 (over z, y), mp: 4 (over x, core).
Axes of the slice: x: 2, y: 2, z: 4, core: 2. Of those that a mesh axis runs over, the one named last changes fastest.
Arguments:
- query_inputs: bfloat16 [128, 28672], P(None, 'mp'), may hold values from -0.09375 to 0.09375
- query_grads: bfloat16 [128, 8192], P(None, 'mp'), may hold values from -6 to 6
- basis_inputs: bfloat16 [28672, 28672], P('mp', 'dp'), may hold values from -0.03125 to 0.03125
- basis_grads: bfloat16 [8192, 8192], P('mp', 'dp'), may hold values from -0.0625 to 0.0625
- eig_inputs: float32 [28672], P('dp'), may hold values from 0.25 to 4
- eig_grads: float32 [8192], P('dp'), may hold values from 0.25 to 4
- train_inputs: bfloat16 [6144, 28672], P('dp', 'mp'), may hold values from -0.03540039 to 0.03540039
- train_grads: bfloat16 [6144, 8192], P('dp', 'mp'), may hold values from -0.06591797 to 0.06591797
Outputs:
- scores: float32 [4, 48], P('mp', 'dp')
The draws below stay inside these ranges and needn't reach their ends.
All inputs are finite; a program needn't handle non-finite values.
Results may differ from the reference program's by a relative error of at most 0.0054.
Values may be sent and summed in bfloat16 or wider, within the bound.
A program may use at most 128 MiB of HBM per device.

```python
import math
import jax
import jax.numpy as jnp
from jax import lax

FA = 28672
FS = 8192
LEN = 128
QLEN = 32
NQ = 4
QT = 128
NSEQ = 48
TRAIN_TOK = 6144


def block_scale(own_key, dims, pieces, smallest, high):
    def one(position, shards_of):
        draws = jax.random.uniform(jax.random.fold_in(jax.random.fold_in(own_key, 6), position), (shards_of,), jnp.float32, smallest / len(pieces), high / len(pieces))
        return jnp.repeat(jnp.exp(draws), dims[position] // shards_of).reshape((-1,) + (1,) * (len(dims) - position - 1))

    gain = one(*pieces[0])
    for cut in pieces[1:]:
        gain = gain * one(*cut)
    return gain


def gaussian(own_key, shape, scale, most, split=(), held_as=jnp.bfloat16):
    drawn = scale * jax.random.normal(own_key, shape, jnp.float32)
    if split:
        drawn = drawn * block_scale(own_key, shape, split, -0.22, 0.18)
    return jnp.clip(drawn, -most, most).astype(held_as)


def setup_inputs(seed: int = 0) -> dict:
    keys = jax.random.split(jax.random.key(seed), 9)
    return {
        "query_inputs": gaussian(keys[0], (QT, FA), ((QLEN * LEN) ** -0.5), 0.09375, ((1, 4),)),
        "query_grads": gaussian(keys[1], (QT, FS), 1.0, 6.0, ((1, 4),)),
        "basis_inputs": gaussian(keys[2], (FA, FA), FA ** -0.5, 0.03125, ((0, 4), (1, 8))),
        "basis_grads": gaussian(keys[3], (FS, FS), FS ** -0.5, 0.0625, ((0, 4), (1, 8))),
        "eig_inputs": jnp.clip(jnp.exp(math.log(4.0) - 2.7725887 * jax.random.uniform(keys[4], (FA,), jnp.float32) ** block_scale(keys[4], (FA,), ((0, 8),), -0.2, 0.2)), 0.25, 4.0),
        "eig_grads": jnp.clip(jnp.exp(math.log(4.0) - 2.7725887 * jax.random.uniform(keys[5], (FS,), jnp.float32) ** block_scale(keys[5], (FS,), ((0, 8),), -0.2, 0.2)), 0.25, 4.0),
        "train_inputs": gaussian(keys[6], (TRAIN_TOK, FA), (FA ** -0.5), 0.03540039, ((0, 8), (1, 4))),
        "train_grads": gaussian(keys[7], (TRAIN_TOK, FS), (FS ** -0.5), 0.06591797, ((0, 8), (1, 4))),
    }


def precondition(factors, basis, eigen):
    rotated = jnp.dot(factors, basis, preferred_element_type=jnp.float32)
    scaled = (rotated / eigen[None, :]).astype(jnp.bfloat16)
    return jnp.dot(scaled, basis.T, preferred_element_type=jnp.float32).astype(jnp.bfloat16)


def reference(query_inputs, query_grads, basis_inputs, basis_grads, eig_inputs, eig_grads, train_inputs, train_grads):
    pre_in = precondition(query_inputs, basis_inputs, eig_inputs)
    pre_out = precondition(query_grads, basis_grads, eig_grads)
    seq_inputs = train_inputs.reshape(NSEQ, LEN, FA)
    seq_grads = train_grads.reshape(NSEQ, LEN, FS)

    def one_sequence(pair):
        seq_in, seq_out = pair
        inner_in = jnp.dot(pre_in, seq_in.T, preferred_element_type=jnp.float32)
        inner_out = jnp.dot(pre_out, seq_out.T, preferred_element_type=jnp.float32)
        products = inner_in * inner_out
        return jnp.sum(products.reshape(NQ, QLEN, LEN), axis=(1, 2))

    per_sequence = lax.map(one_sequence, (seq_inputs, seq_grads))
    return per_sequence.T
```

```python
import functools
import math

import jax
import jax.numpy as jnp
from jax import lax
from jax.experimental import pallas as pl
from jax.experimental.pallas import tpu as pltpu
from jax.sharding import PartitionSpec as P

LEN = 128
QLEN = 32
WSLOTS = 4
TSLOTS = 3
F32 = jnp.float32
BF16 = jnp.bfloat16
NT = (((1,), (1,)), ((), ()))


def bit_count(size):
    return size.bit_length() - 1


def reverse_bits(value, bits):
    out = 0
    for _ in range(bits):
        out, value = out * 2 + value % 2, value // 2
    return out


def kernel(
    dims,
    qin, qout, ein, eout, bin_, bout, tin, tout,
    out,
    w, tr, acc1, rb1, scaled, acc2, sb2, rb2, pre, inner, rbc,
    wsem, tsem, s1, r1, s2, r2, sc, rc,
):
    rows, fc, cc, tokens, n_in, n_out, dp, mp = dims
    nd, nm = bit_count(dp), bit_count(mp)
    chunks = n_out + n_in
    d, m = lax.axis_index("dp"), lax.axis_index("mp")
    pending = []

    def bit_of(axis, b):
        return lax.rem((d if axis == "dp" else m) // (2**b), 2)

    def partner(axis, b):
        return {axis: (d if axis == "dp" else m) + 2**b * (1 - 2 * bit_of(axis, b))}

    def hint(x, size):
        return pl.multiple_of(x, size)

    def remote(src, dst, ssem, rsem, axis, b):
        copy = pltpu.make_async_remote_copy(
            src_ref=src, dst_ref=dst, send_sem=ssem, recv_sem=rsem,
            device_id=partner(axis, b), device_id_type=pl.DeviceIdType.MESH,
        )
        copy.start()
        pending.append(copy)
        return copy

    def tile_copies(t):
        slot = t % WSLOTS
        c = t % chunks
        base, local, count = (bout, c, n_out) if c < n_out else (bin_, c - n_out, n_in)
        if t < chunks:
            return [
                pltpu.make_async_copy(
                    base.at[:, pl.ds(local * cc, cc)],
                    w.at[slot, pl.ds(0, count * fc)],
                    wsem.at[slot, 0],
                )
            ]
        return [
            pltpu.make_async_copy(
                base.at[pl.ds(local * fc, fc), pl.ds(k * cc, cc)],
                w.at[slot, pl.ds(k * fc, fc)],
                wsem.at[slot, k],
            )
            for k in range(count)
        ]

    def tile_start(t):
        if t < 2 * chunks:
            for copy in tile_copies(t):
                copy.start()

    def tile_wait(t):
        for copy in tile_copies(t):
            copy.wait()

    def train_copy(c):
        base, local = (tout, c) if c < n_out else (tin, c - n_out)
        return pltpu.make_async_copy(
            base.at[:, pl.ds(local * fc, fc)], tr.at[c % TSLOTS], tsem.at[c % TSLOTS]
        )

    for t in range(WSLOTS):
        tile_start(t)

    barrier = pltpu.get_barrier_semaphore()
    for axis, bits in (("dp", nd), ("mp", nm)):
        for b in range(bits):
            pl.semaphore_signal(
                barrier, inc=1, device_id=partner(axis, b),
                device_id_type=pl.DeviceIdType.MESH,
            )
    pl.semaphore_wait(barrier, nd + nm)

    for c in range(min(TSLOTS, chunks)):
        train_copy(c).start()

    def rotate(c):
        slot = c % WSLOTS
        tile_wait(c)
        lhs, count = (qout, n_out) if c < n_out else (qin, n_in)
        acc1[c] = jnp.zeros((rows, cc), F32)

        def step(k, carry):
            at = pl.ds(hint(k * fc, fc), fc)
            acc1[c] += jnp.dot(lhs[:, at], w[slot, at, :], preferred_element_type=F32)
            return carry

        lax.fori_loop(0, count, step, 0)
        tile_start(c + WSLOTS)

    def first(c):
        rotate(c)
        yield
        lo, size, trail = 0, rows, []
        off = 0
        for k in range(nm):
            half = size // 2
            bit = bit_of("mp", k)
            give = hint(lo + (1 - bit) * half, half)
            trail.append(lo)
            copy = remote(
                acc1.at[c, pl.ds(give, half)], rb1.at[c, pl.ds(off, half)],
                s1.at[c, k], r1.at[c, k], "mp", k,
            )
            lo = hint(lo + bit * half, half)
            size = half
            yield
            copy.wait_recv()
            if k < nm - 1:
                acc1[c, pl.ds(lo, half)] += rb1[c, pl.ds(off, half)]
            else:
                eig, local = (eout, c) if c < n_out else (ein, c - n_out)
                total = acc1[c, pl.ds(lo, half)] + rb1[c, pl.ds(off, half)]
                scaled[c, pl.ds(lo, half)] = (
                    total / eig[:, pl.ds(local * cc, cc)]
                ).astype(BF16)
            off += half
        for k in reversed(range(nm)):
            part = scaled.at[c, pl.ds(lo, size)]
            copy = remote(part, part, s1.at[c, nm + k], r1.at[c, nm + k], "mp", k)
            lo = trail[k] if k == 0 else hint(trail[k], size * 2)
            size *= 2
            yield
            copy.wait_recv()

    def rotate_back(c):
        t = chunks + c
        slot = t % WSLOTS
        tile_wait(t)
        start, count = (0, n_out) if c < n_out else (n_out, n_in)
        acc2[c] = jnp.zeros((rows, fc), F32)

        def step(k, carry):
            acc2[c] += lax.dot_general(
                scaled[start + k], w[slot, pl.ds(hint(k * fc, fc), fc), :], NT,
                preferred_element_type=F32,
            )
            return carry

        lax.fori_loop(0, count, step, 0)
        tile_start(t + WSLOTS)

    def second(c):
        rotate_back(c)
        order = list(range(nd))
        if c % 2 and nd > 1:
            order[0], order[1] = order[1], order[0]
        lo, size, trail = 0, rows, []
        off = 0
        for k, b in enumerate(order):
            half = size // 2
            bit = bit_of("dp", b)
            give = hint(lo + (1 - bit) * half, half)
            trail.append(lo)
            sb2[c, pl.ds(off, half)] = acc2[c, pl.ds(give, half)].astype(BF16)
            copy = remote(
                sb2.at[c, pl.ds(off, half)], rb2.at[c, pl.ds(off, half)],
                s2.at[c, k], r2.at[c, k], "dp", b,
            )
            lo = hint(lo + bit * half, half)
            size = half
            yield
            copy.wait_recv()
            total = acc2[c, pl.ds(lo, half)] + rb2[c, pl.ds(off, half)].astype(F32)
            if k < nd - 1:
                acc2[c, pl.ds(lo, half)] = total
            else:
                pre[c, pl.ds(lo, half)] = total.astype(BF16)
            off += half
        for k in reversed(range(nd)):
            part = pre.at[c, pl.ds(lo, size)]
            copy = remote(part, part, s2.at[c, nd + k], r2.at[c, nd + k], "dp", order[k])
            lo = trail[k] if k == 0 else hint(trail[k], size * 2)
            size *= 2
            yield
            copy.wait_recv()
        train_copy(c).wait()
        found = lax.dot_general(
            pre[c], tr[c % TSLOTS], NT, preferred_element_type=F32
        )
        if c + TSLOTS < chunks:
            train_copy(c + TSLOTS).start()
        side = 0 if c < n_out else 1
        block = rows // mp
        for i in range(mp):
            at = pl.ds(reverse_bits(i, nm) * block, block)
            piece = found[i * block : (i + 1) * block]
            if c == 0 or c == n_out:
                inner[side, at] = piece
            else:
                inner[side, at] += piece

    def third(side):
        lo, size, off = 0, rows, 0
        for k in range(nm):
            half = size // 2
            bit = bit_of("mp", k)
            give = hint(lo + (1 - bit) * half, half)
            copy = remote(
                inner.at[side, pl.ds(give, half)], rbc.at[side, pl.ds(off, half)],
                sc.at[side, k], rc.at[side, k], "mp", k,
            )
            lo = hint(lo + bit * half, half)
            size = half
            yield
            copy.wait_recv()
            inner[side, pl.ds(lo, half)] += rbc[side, pl.ds(off, half)]
            off += half
        result.append(inner[side, pl.ds(lo, size)])

    result = []
    live = []

    def turn(fresh=None):
        if fresh is not None:
            next(fresh)
        for item in list(live):
            if next(item, "done") == "done":
                live.remove(item)
        if fresh is not None:
            live.append(fresh)

    for c in range(chunks):
        turn(first(c))
    early = []
    for c in range(n_out):
        item = second(c)
        turn(item)
        early.append(item)
    while any(item not in early for item in live):
        turn()
    outer = None
    for c in range(n_out, chunks):
        turn(second(c))
        if outer is None and not any(item in live for item in early):
            outer = third(0)
            next(outer)
            live.append(outer)
    while live:
        turn()
        if outer is None and not any(item in live for item in early):
            outer = third(0)
            next(outer)
            live.append(outer)
    for _ in third(1):
        pass
    products = result[0] * result[1]
    block = rows // mp
    cells = lax.broadcasted_iota(jnp.int32, out.shape, 1)
    lines = lax.broadcasted_iota(jnp.int32, out.shape, 0)
    answer = jnp.zeros(out.shape, F32)
    for i in range(block // QLEN):
        for n in range(tokens // LEN):
            part = products[i * QLEN : (i + 1) * QLEN, n * LEN : (n + 1) * LEN]
            value = jnp.sum(jnp.sum(part, axis=0, keepdims=True), axis=1, keepdims=True)
            answer = jnp.where((cells == n) & (lines == i), value, answer)
    out[...] = answer
    for copy in pending:
        copy.wait_send()


def per_device(
    dp, mp,
    query_inputs, query_grads, basis_inputs, basis_grads,
    eig_inputs, eig_grads, train_inputs, train_grads,
):
    rows = query_inputs.shape[0]
    feat_in, cols_in = basis_inputs.shape
    feat_out, cols_out = basis_grads.shape
    tokens = train_inputs.shape[0]
    fc = math.gcd(feat_in, feat_out)
    n_in, n_out = feat_in // fc, feat_out // fc
    cc = cols_in // n_in
    nd, nm = bit_count(dp), bit_count(mp)
    chunks = n_in + n_out
    dims = (rows, fc, cc, tokens, n_in, n_out, dp, mp)
    vmem = pl.BlockSpec(memory_space=pltpu.VMEM)
    hbm = pl.BlockSpec(memory_space=pl.ANY)
    dma = pltpu.SemaphoreType.DMA
    return pl.pallas_call(
        functools.partial(kernel, dims),
        out_shape=jax.ShapeDtypeStruct((rows // mp // QLEN, tokens // LEN), F32),
        in_specs=[vmem] * 4 + [hbm] * 4,
        out_specs=vmem,
        scratch_shapes=[
            pltpu.VMEM((WSLOTS, feat_in, cc), BF16),
            pltpu.VMEM((TSLOTS, tokens, fc), BF16),
            pltpu.VMEM((chunks, rows, cc), F32),
            pltpu.VMEM((chunks, rows - rows // mp, cc), F32),
            pltpu.VMEM((chunks, rows, cc), BF16),
            pltpu.VMEM((chunks, rows, fc), F32),
            pltpu.VMEM((chunks, rows - rows // dp, fc), BF16),
            pltpu.VMEM((chunks, rows - rows // dp, fc), BF16),
            pltpu.VMEM((chunks, rows, fc), BF16),
            pltpu.VMEM((2, rows, tokens), F32),
            pltpu.VMEM((2, rows - rows // mp, tokens), F32),
            dma((WSLOTS, n_in)),
            dma((TSLOTS,)),
            dma((chunks, 2 * nm)),
            dma((chunks, 2 * nm)),
            dma((chunks, 2 * nd)),
            dma((chunks, 2 * nd)),
            dma((2, nm)),
            dma((2, nm)),
        ],
        compiler_params=pltpu.CompilerParams(
            collective_id=0, has_side_effects=True, vmem_limit_bytes=66000000
        ),
    )(
        query_inputs, query_grads, eig_inputs[None, :], eig_grads[None, :],
        basis_inputs, basis_grads, train_inputs, train_grads,
    )


def solution(mesh):
    return jax.shard_map(
        functools.partial(per_device, mesh.shape["dp"], mesh.shape["mp"]),
        mesh=mesh,
        in_specs=(
            P(None, "mp"),
            P(None, "mp"),
            P("mp", "dp"),
            P("mp", "dp"),
            P("dp"),
            P("dp"),
            P("dp", "mp"),
            P("dp", "mp"),
        ),
        out_specs=P("mp", "dp"),
        check_vma=False,
    )
```
